32 devices in a mesh: span: 16 (over z, x, core), qry: 2 (over y).
Axes of the slice: x: 2, y: 2, z: 4, core: 2. Of those that a mesh axis runs over, the one named last changes fastest.
Arguments:
- features: bfloat16 [16, 4, 128, 256], P('span', 'qry'), may hold values from -6 to 6
- conv_weight: bfloat16 [27, 256, 256], replicated, may hold values from -0.078125 to 0.078125
- queries: float32 [16, 256], P('qry'), may hold values from -600 to 600
- w_query: bfloat16 [2, 256, 256], replicated, may hold values from -0.26171875 to 0.26171875
- w_key: bfloat16 [2, 256, 256], replicated, may hold values from -0.26171875 to 0.26171875
- w_value: bfloat16 [2, 256, 256], replicated, may hold values from -0.26171875 to 0.26171875
- w_out: bfloat16 [2, 256, 256], replicated, may hold values from -0.26171875 to 0.26171875
- norm_gain: float32 [256], replicated, may hold values from 0.5 to 1.5
- mask_weight: bfloat16 [256, 256], replicated, may hold values from -0.375 to 0.375
- mask_blocks: int32 [16, 4], replicated, may hold values from 0 to 63, as said below
Outputs:
- query_embed: float32 [16, 256], P('qry')
- mask_logits: bfloat16 [16, 16, 4, 128], P(None, 'span', 'qry')
The draws below stay inside these ranges and needn't reach their ends.
Inputs may be any that keep to these rules, and one draw needn't show every extreme that they name: `mask_blocks`: each row lists 4 distinct mask blocks, block z * 4 + y being the voxels pixel[z, y, :]; no block appears twice in the whole array.
All inputs are finite; a program needn't handle non-finite values.
Results may differ from the reference program's by a relative error of at most 0.04.
The reference program's roundings to bfloat16 on the way (of `pixel`, `qproj`, `attn` and `mask_embed`) count: a program that leaves them out, or rounds other values in their place, can miss the bound.
Values may be sent and summed in bfloat16 or wider, within the bound.
No kernel may reach another device: no remote copies, remote signals or barrier semaphores. Data moves between devices by JAX's collectives and lax.ppermute only.
A program may use at most 64 MiB of HBM per device.

```python
import jax
import jax.numpy as jnp
from jax import lax

D = 256
HEADS = 8
HEAD_DIM = 32
LAYERS = 2
MB = 4
NX = 128
NZ = 16
NY = 4
NBLK = 64
NQ = 16


def draw_queries(key, part):
    first_key = jax.random.fold_in(key, 0)
    values = jnp.clip(jax.random.normal(first_key, (NQ, D), jnp.float32), -6.0, 6.0)
    return values.astype(jnp.float32)


def draw_mask_blocks(key, part):
    order = jax.random.permutation(jax.random.fold_in(key, 17), NBLK)
    return order[:NQ * MB].reshape(NQ, MB).astype(jnp.int32)


def block_levels(rng, dims, shards, smallest, largest):
    gain, own = 1.0, jax.random.fold_in(rng, 6)
    for dim, blocks in shards:
        heights = jnp.exp(jax.random.uniform(jax.random.fold_in(own, dim), (blocks,), jnp.float32, smallest / len(shards), largest / len(shards)))
        gain = gain * jnp.repeat(heights, dims[dim] // blocks).reshape([-1 if axis == dim else 1 for axis in range(len(dims))])
    return gain


def bell_draw(stream_key, shape, width, reach, pieces=(), held_as=jnp.bfloat16):
    gain = block_levels(stream_key, shape, pieces, -0.22, 0.18) if pieces else 1.0
    drawn = jax.random.normal(stream_key, shape, jnp.float32) * width * gain
    return jnp.minimum(jnp.maximum(drawn, -reach), reach).astype(held_as)


def setup_inputs(seed: int = 0) -> dict:
    seeds = jax.random.split(jax.random.key(seed), 11)
    return {
        "features": bell_draw(seeds[0], (NZ, NY, NX, D), 1.0, 6.0, ((0, 16), (1, 2))),
        "conv_weight": bell_draw(seeds[1], (27, D, D), (27 * D) ** -0.5, 0.078125),
        "queries": draw_queries(jax.random.fold_in(seeds[10], 71), 0),
        "w_query": jnp.clip(jax.random.uniform(seeds[3], (LAYERS, D, D), jnp.float32, -0.26171875, 0.26171875), -0.26171875, 0.26171875).astype(jnp.bfloat16),
        "w_key": jnp.clip(jax.random.uniform(seeds[4], (LAYERS, D, D), jnp.float32, -0.26171875, 0.26171875), -0.26171875, 0.26171875).astype(jnp.bfloat16),
        "w_value": jnp.clip(jax.random.uniform(seeds[5], (LAYERS, D, D), jnp.float32, -0.26171875, 0.26171875), -0.26171875, 0.26171875).astype(jnp.bfloat16),
        "w_out": jnp.clip(jax.random.uniform(seeds[6], (LAYERS, D, D), jnp.float32, -0.26171875, 0.26171875), -0.26171875, 0.26171875).astype(jnp.bfloat16),
        "norm_gain": jnp.clip(1.0 + 0.1 * jax.random.normal(seeds[7], (D,), jnp.float32), 0.5, 1.5),
        "mask_weight": bell_draw(seeds[8], (D, D), D ** -0.5, 0.375),
        "mask_blocks": draw_mask_blocks(jax.random.fold_in(seeds[10], 71), 0),
    }


def reference(features, conv_weight, queries, w_query, w_key, w_value, w_out, norm_gain, mask_weight, mask_blocks):
    padded = jnp.pad(features, ((1, 1), (1, 1), (1, 1), (0, 0)))

    def plane(z_index):
        slab = lax.dynamic_slice_in_dim(padded, z_index, 3, 0)
        total = jnp.zeros((NY * NX, D), jnp.float32)
        for depth_off in range(3):
            for row_off in range(3):
                for col_off in range(3):
                    tap = slab[depth_off, row_off:row_off + NY, col_off:col_off + NX].reshape(NY * NX, D)
                    total = total + jnp.dot(tap, conv_weight[9 * depth_off + 3 * row_off + col_off], preferred_element_type=jnp.float32)
        return jnp.maximum(total, 0.0).astype(jnp.bfloat16).reshape(NY, NX, D)
    pixel = lax.map(plane, jnp.arange(NZ, dtype=jnp.int32))
    flat = pixel.reshape(NZ * NY * NX, D)
    state = queries
    scale = HEAD_DIM ** (-0.5)
    for layer_index in range(LAYERS):
        qproj = (jnp.dot(state.astype(jnp.bfloat16), w_query[layer_index], preferred_element_type=jnp.float32) * scale).astype(jnp.bfloat16)
        keys = jnp.dot(flat, w_key[layer_index], preferred_element_type=jnp.float32).astype(jnp.bfloat16).reshape(NBLK, NX, D)
        values = jnp.dot(flat, w_value[layer_index], preferred_element_type=jnp.float32).astype(jnp.bfloat16).reshape(NBLK, NX, D)
        picked_keys = keys[mask_blocks].reshape(NQ, MB * NX, HEADS, HEAD_DIM).astype(jnp.float32)
        picked_values = values[mask_blocks].reshape(NQ, MB * NX, HEADS, HEAD_DIM).astype(jnp.float32)
        scores = jnp.einsum('nhe,nvhe->nhv', qproj.reshape(NQ, HEADS, HEAD_DIM).astype(jnp.float32), picked_keys)
        top = lax.optimization_barrier(jnp.max(scores, axis=-1, keepdims=True))
        prob = jnp.exp(scores - top)
        total = lax.optimization_barrier(jnp.sum(prob, axis=-1))
        weighted = jnp.einsum('nhv,nvhe->nhe', prob.astype(jnp.bfloat16).astype(jnp.float32), picked_values)
        attn = (weighted / total[:, :, None]).reshape(NQ, D).astype(jnp.bfloat16)
        state = state + jnp.dot(attn, w_out[layer_index], preferred_element_type=jnp.float32)
    mean = lax.optimization_barrier(jnp.mean(state, axis=-1, keepdims=True))
    centered = state - mean
    var = lax.optimization_barrier(jnp.mean(centered * centered, axis=-1, keepdims=True))
    query_embed = centered * lax.rsqrt(var + 1e-05) * norm_gain
    mask_embed = jnp.dot(query_embed.astype(jnp.bfloat16), mask_weight, preferred_element_type=jnp.float32).astype(jnp.bfloat16)
    logits = jnp.einsum('nd,vd->nv', mask_embed, flat, preferred_element_type=jnp.float32) * D ** (-0.5)
    mask_logits = logits.astype(jnp.bfloat16).reshape(NQ, NZ, NY, NX)
    return (query_embed, mask_logits)
```

```python
import functools

import jax
import jax.numpy as jnp
from jax import lax
from jax.experimental import pallas as pl
from jax.experimental.pallas import tpu as pltpu
from jax.sharding import PartitionSpec as P

HEADS = 8
LAYERS = 2
LANES = 128
SLOTS = 8
F32 = jnp.float32
BF16 = jnp.bfloat16
EXACT = lax.Precision.HIGHEST


def iota(shape, dim):
    return lax.broadcasted_iota(jnp.int32, shape, dim)


def swap_partner(index, count, parity):
    other = index ^ 1 if parity == 0 else ((index + 1) ^ 1) - 1
    return other if 0 <= other < count else None


def swap(value, axes, counts, parities):
    pairs = []
    for first in range(counts[0]):
        for second in range(counts[1]):
            ends = [
                index if parity is None else swap_partner(index, count, parity)
                for index, count, parity in zip((first, second), counts, parities)
            ]
            if None not in ends:
                pairs.append((first * counts[1] + second, ends[0] * counts[1] + ends[1]))
    return lax.ppermute(value, axes, pairs)


def partials(qproj, keys, values, mask_rows, base, x_cells, out_ref):
    voxels, channels = keys.shape
    query_count = qproj.shape[0]
    blocks = voxels // x_cells
    rows = blocks * HEADS
    head_dim = channels // HEADS
    block_of_row = base + iota((rows, query_count), 0) // HEADS
    listed = mask_rows[0:1, :] == block_of_row
    for place in range(1, mask_rows.shape[0]):
        listed = listed | (mask_rows[place : place + 1, :] == block_of_row)
    chosen = jnp.dot(listed.astype(F32).astype(BF16), qproj, preferred_element_type=F32)
    own_head = iota((rows, channels), 1) // head_dim == iota((rows, channels), 0) % HEADS
    chosen = jnp.where(own_head, chosen, 0.0).astype(BF16)
    scores = lax.dot_general(chosen, keys, (((1,), (1,)), ((), ())), preferred_element_type=F32)
    allowed = iota((rows, voxels), 1) // x_cells == iota((rows, voxels), 0) // HEADS
    top = jnp.max(jnp.where(allowed, scores, -jnp.inf), axis=1, keepdims=True)
    prob = jnp.where(allowed, jnp.exp(scores - top), 0.0)
    total = jnp.sum(prob, axis=1, keepdims=True)
    weighted = jnp.dot(prob.astype(BF16), values, preferred_element_type=F32)
    weighted = jnp.where(own_head, weighted, 0.0)
    lane_head = iota((rows, LANES), 1) == iota((rows, LANES), 0) % HEADS
    top = jnp.where(lane_head, top, 0.0)
    total = jnp.where(lane_head, total, 0.0)
    wide = channels // LANES
    for block in range(blocks):
        span = slice(block * HEADS, (block + 1) * HEADS)
        summed = jnp.sum(weighted[span], axis=0, keepdims=True)
        for part in range(wide):
            row = block * wide + part
            out_ref[row : row + 1, :] = summed[:, part * LANES : (part + 1) * LANES]
        row = blocks * wide + block
        out_ref[row : row + 1, :] = jnp.sum(top[span], axis=0, keepdims=True)
        row = blocks * (wide + 1) + block
        out_ref[row : row + 1, :] = jnp.sum(total[span], axis=0, keepdims=True)


def merged(parts_ref, mask_column, blocks, channels, query_count):
    wide = channels // LANES
    slots = blocks * (wide + 2)
    devices = parts_ref.shape[0] // slots
    listed = mask_column.shape[0]
    places = listed // query_count

    def slot(index):
        return parts_ref[pl.ds(index, devices, stride=slots), :]

    by_block = jnp.concatenate(
        [
            jnp.concatenate(
                [slot(block * wide + part) for part in range(wide)]
                + [slot(blocks * wide + block), slot(blocks * (wide + 1) + block)],
                axis=1,
            )
            for block in range(blocks)
        ],
        axis=0,
    )
    column = iota((listed, devices * blocks), 1)
    block_id = (column % devices) * blocks + column // devices
    pick = (mask_column == block_id).astype(F32)
    picked = jnp.dot(pick, by_block, precision=EXACT, preferred_element_type=F32)

    def place(index, start, size):
        return picked[index * query_count : (index + 1) * query_count, start : start + size]

    tops = [place(index, channels, LANES) for index in range(places)]
    totals = [place(index, channels + LANES, LANES) for index in range(places)]
    top = functools.reduce(jnp.maximum, tops)
    factors = [jnp.exp(part - top) for part in tops]
    total = sum(factor * part for factor, part in zip(factors, totals))
    valid = iota((query_count, LANES), 1) < HEADS
    shares = [jnp.where(valid, factor / total, 0.0) for factor in factors]
    spread = (
        iota((LANES, channels), 1) // (channels // HEADS) == iota((LANES, channels), 0)
    ).astype(F32)
    wide_shares = jnp.dot(
        jnp.concatenate(shares, axis=0), spread, precision=EXACT, preferred_element_type=F32
    )
    attn = sum(
        wide_shares[index * query_count : (index + 1) * query_count] * place(index, 0, channels)
        for index in range(places)
    )
    return attn.astype(BF16)


def project(state, w_query, head_dim):
    return (
        jnp.dot(state.astype(BF16), w_query, preferred_element_type=F32) * head_dim ** (-0.5)
    ).astype(BF16)


def conv_kernel(rows_out, *refs):
    (own, plane_even, plane_odd, *rest) = refs
    halos = rest[: 3 * rows_out]
    (taps_hbm, queries, peers, w_query, w_key, w_value, mask_rows) = rest[
        3 * rows_out : 3 * rows_out + 7
    ]
    (pixel, states, parts, cells, taps, arrived) = rest[3 * rows_out + 7 :]
    row_cells, x_cells, channels = own.shape
    depth_id = lax.axis_index("span")
    row_id = lax.axis_index("qry")
    copies = []
    for depth_off in range(3):
        chunk = pl.ds(9 * depth_off, 9)
        copies.append(
            pltpu.make_async_copy(taps_hbm.at[chunk], taps.at[chunk], arrived.at[depth_off])
        )
        copies[-1].start()
    odd = depth_id % 2
    even_plane = 2 - 2 * odd
    odd_plane = 2 * odd
    blank = jnp.zeros((x_cells, channels), BF16)
    for depth_off in range(3):
        cells[depth_off, 0] = blank
        cells[depth_off, row_cells + 1] = blank
    for row in range(row_cells):
        cells[1, row + 1] = own[row]
        cells[even_plane, row + 1] = plane_even[row]
        cells[odd_plane, row + 1] = plane_odd[row]
    low = row_id % 2 == 0
    for parity in range(rows_out):
        at_end = low if parity == 0 else jnp.logical_not(low)
        row = jnp.where(at_end, row_cells + 1, 0)
        cells[1, row] = halos[3 * parity][...]
        cells[even_plane, row] = halos[3 * parity + 1][...]
        cells[odd_plane, row] = halos[3 * parity + 2][...]
    voxels = row_cells * x_cells
    sums = [None, None, None]
    for depth_off in range(3):
        copies[depth_off].wait()
        for row_off in range(3):
            slab = cells[depth_off, row_off : row_off + row_cells].reshape(voxels, channels)
            for x_off in range(3):
                product = jnp.dot(
                    slab, taps[9 * depth_off + 3 * row_off + x_off], preferred_element_type=F32
                )
                sums[x_off] = product if sums[x_off] is None else sums[x_off] + product
    x_id = iota((voxels, channels), 0) % x_cells
    conv = (
        sums[1]
        + jnp.where(x_id == 0, 0.0, pltpu.roll(sums[0], 1, 0))
        + jnp.where(x_id == x_cells - 1, 0.0, pltpu.roll(sums[2], voxels - 1, 0))
    )
    flat = jnp.maximum(conv, 0.0).astype(BF16)
    pixel[...] = flat
    here = queries.shape[0]
    if peers.shape[0] == states.shape[0]:
        states[...] = peers[...]
    else:
        states[pl.ds(pl.multiple_of(row_id * here, here), here), :] = queries[...]
        states[pl.ds(pl.multiple_of((1 - row_id) * here, here), here), :] = peers[...]
    qproj = project(states[...], w_query[0], channels // HEADS)
    keys = jnp.dot(flat, w_key[0], preferred_element_type=F32).astype(BF16)
    values = jnp.dot(flat, w_value[0], preferred_element_type=F32).astype(BF16)
    base = (depth_id * lax.axis_size("qry") + row_id) * row_cells
    partials(qproj, keys, values, mask_rows[...], base, x_cells, parts)


def layer_kernel(
    layer,
    x_cells,
    pixel,
    states,
    gathered,
    w_out,
    w_query,
    w_key,
    w_value,
    mask_rows,
    mask_column,
    new_states,
    parts,
):
    voxels, channels = pixel.shape
    blocks = voxels // x_cells
    flat = pixel[...]
    keys = jnp.dot(flat, w_key[layer], preferred_element_type=F32).astype(BF16)
    values = jnp.dot(flat, w_value[layer], preferred_element_type=F32).astype(BF16)
    attn = merged(gathered, mask_column[...], blocks, channels, states.shape[0])
    state = states[...] + jnp.dot(attn, w_out[layer - 1], preferred_element_type=F32)
    new_states[...] = state
    qproj = project(state, w_query[layer], channels // HEADS)
    base = (lax.axis_index("span") * lax.axis_size("qry") + lax.axis_index("qry")) * blocks
    partials(qproj, keys, values, mask_rows[...], base, x_cells, parts)


def final_kernel(
    x_cells, pixel, states, gathered, w_out, norm_gain, mask_weight, mask_column, embed, logits, all_rows
):
    voxels, channels = pixel.shape
    blocks = voxels // x_cells
    attn = merged(gathered, mask_column[...], blocks, channels, states.shape[0])
    state = states[...] + jnp.dot(attn, w_out[LAYERS - 1], preferred_element_type=F32)
    mean = jnp.mean(state, axis=-1, keepdims=True)
    centered = state - mean
    var = jnp.mean(centered * centered, axis=-1, keepdims=True)
    query_embed = centered * lax.rsqrt(var + 1e-05) * norm_gain[...]
    all_rows[...] = query_embed
    here = embed.shape[0]
    embed[...] = all_rows[pl.ds(pl.multiple_of(lax.axis_index("qry") * here, here), here), :]
    mask_embed = jnp.dot(
        query_embed.astype(BF16), mask_weight[...], preferred_element_type=F32
    ).astype(BF16)
    scores = lax.dot_general(
        mask_embed, pixel[...], (((1,), (1,)), ((), ())), preferred_element_type=F32
    ) * channels ** (-0.5)
    for block in range(blocks):
        logits[:, block, :] = scores[:, block * x_cells : (block + 1) * x_cells].astype(BF16)


def shape(dims, dtype):
    return jax.ShapeDtypeStruct(dims, dtype)


VMEM = pl.BlockSpec(memory_space=pltpu.VMEM)
ANY = pl.BlockSpec(memory_space=pl.ANY)


def exchange(parts, devices):
    axes = ("span", "qry")
    copies = jnp.broadcast_to(parts[None], (devices, *parts.shape))
    gathered = lax.all_to_all(copies, axes, split_axis=0, concat_axis=0, tiled=True)
    return gathered.reshape(devices * parts.shape[0], LANES)


def local(
    counts,
    features,
    conv_weight,
    queries,
    w_query,
    w_key,
    w_value,
    w_out,
    norm_gain,
    mask_weight,
    mask_blocks,
):
    depth_cells, row_cells, x_cells, channels = features.shape
    assert depth_cells == 1
    axes = ("span", "qry")
    devices = counts[0] * counts[1]
    query_count, places = mask_blocks.shape
    voxels = row_cells * x_cells
    slots = row_cells * (channels // LANES + 2)
    own = features[0]
    plane_odd = swap(own, axes, counts, (1, None))
    plane_even = swap(own, axes, counts, (0, None))
    row_low = lax.axis_index("qry") % 2 == 0
    halos = []
    parities = (0,) if counts[1] == 2 else (0, 1)
    for parity in parities:
        at_end = row_low if parity == 0 else jnp.logical_not(row_low)
        edge = lax.dynamic_index_in_dim(
            own, jnp.where(at_end, row_cells - 1, 0), axis=0, keepdims=False
        )
        row = swap(edge, axes, counts, (None, parity))
        corner_odd = swap(edge, axes, counts, (1, parity))
        corner_even = swap(row, axes, counts, (0, None))
        halos += [row, corner_even, corner_odd]
    if counts[1] == 2:
        peers = swap(queries, axes, counts, (None, 0))
    else:
        peers = lax.all_gather(queries, "qry", axis=0, tiled=True)
    mask_rows = mask_blocks.T
    mask_column = mask_rows.reshape(places * query_count, 1)
    pixel, states, parts = pl.pallas_call(
        functools.partial(conv_kernel, len(parities)),
        out_shape=(
            shape((voxels, channels), BF16),
            shape((query_count, channels), F32),
            shape((slots, LANES), F32),
        ),
        in_specs=[VMEM] * (3 + len(halos)) + [ANY] + [VMEM] * 6,
        out_specs=[VMEM] * 3,
        scratch_shapes=[
            pltpu.VMEM((3, row_cells + 2, x_cells, channels), BF16),
            pltpu.VMEM(conv_weight.shape, BF16),
            pltpu.SemaphoreType.DMA((3,)),
        ],
        name="conv_partials",
    )(
        own,
        plane_even,
        plane_odd,
        *halos,
        conv_weight,
        queries,
        peers,
        w_query,
        w_key,
        w_value,
        mask_rows,
    )
    for layer in range(1, LAYERS):
        states, parts = pl.pallas_call(
            functools.partial(layer_kernel, layer, x_cells),
            out_shape=(shape((query_count, channels), F32), shape((slots, LANES), F32)),
            in_specs=[VMEM] * 9,
            out_specs=[VMEM] * 2,
            name="layer_partials",
        )(
            pixel,
            states,
            exchange(parts, devices),
            w_out,
            w_query,
            w_key,
            w_value,
            mask_rows,
            mask_column,
        )
    embed, logits = pl.pallas_call(
        functools.partial(final_kernel, x_cells),
        out_shape=(
            shape(queries.shape, F32),
            shape((query_count, row_cells, x_cells), BF16),
        ),
        in_specs=[VMEM] * 7,
        out_specs=[VMEM] * 2,
        scratch_shapes=[pltpu.VMEM((query_count, channels), F32)],
        name="final_logits",
    )(
        pixel,
        states,
        exchange(parts, devices),
        w_out,
        norm_gain.reshape(1, channels),
        mask_weight,
        mask_column,
    )
    return embed, logits.reshape(query_count, depth_cells, row_cells, x_cells)


def solution(mesh):
    counts = (mesh.shape["span"], mesh.shape["qry"])
    return jax.shard_map(
        functools.partial(local, counts),
        mesh=mesh,
        in_specs=(
            P("span", "qry", None, None),
            P(),
            P("qry", None),
            P(),
            P(),
            P(),
            P(),
            P(),
            P(),
            P(),
        ),
        out_specs=(P("qry", None), P(None, "span", "qry", None)),
        check_vma=False,
    )
```

```python
import functools

import jax
import jax.numpy as jnp
from jax import lax
from jax.experimental import pallas as pl
from jax.experimental.pallas import tpu as pltpu
from jax.sharding import PartitionSpec as P

HEADS = 8
LAYERS = 2
LANES = 128
SLOTS = 8
PIECES = 3
AXES = ("span", "qry")
F32 = jnp.float32
BF16 = jnp.bfloat16


def iota(dims, dim):
    return lax.broadcasted_iota(jnp.int32, dims, dim)


def swap_partner(index, count, parity):
    other = index ^ 1 if parity == 0 else ((index + 1) ^ 1) - 1
    return other if 0 <= other < count else None


def swap(value, counts, parities):
    pairs = []
    for first in range(counts[0]):
        for second in range(counts[1]):
            ends = [
                index if parity is None else swap_partner(index, count, parity)
                for index, count, parity in zip((first, second), counts, parities)
            ]
            if None not in ends:
                pairs.append((first * counts[1] + second, ends[0] * counts[1] + ends[1]))
    return lax.ppermute(value, AXES, pairs)


def partials(qproj, keys, values, listed, x_cells, slots, out_ref):
    voxels, channels = keys.shape
    blocks = voxels // x_cells
    rows = blocks * HEADS
    head_dim = channels // HEADS
    chosen = jnp.dot(listed, qproj, preferred_element_type=F32)
    own_head = iota((rows, channels), 1) // head_dim == iota((rows, channels), 0) % HEADS
    chosen = jnp.where(own_head, chosen, 0.0).astype(BF16)
    scores = lax.dot_general(chosen, keys, (((1,), (1,)), ((), ())), preferred_element_type=F32)
    allowed = iota((rows, voxels), 1) // x_cells == iota((rows, voxels), 0) // HEADS
    top = jnp.max(jnp.where(allowed, scores, -jnp.inf), axis=1, keepdims=True)
    prob = jnp.where(allowed, jnp.exp(scores - top), 0.0)
    total = jnp.sum(prob, axis=1, keepdims=True)
    weighted = jnp.dot(prob.astype(BF16), values, preferred_element_type=F32)
    weighted = jnp.where(own_head, weighted / total, 0.0)
    rest = top + jnp.log(total)
    lane = iota((rows, LANES), 1)
    head = iota((rows, LANES), 0) % HEADS
    levels = jnp.zeros((rows, LANES), F32)
    for piece in range(PIECES):
        part = rest.astype(BF16).astype(F32)
        rest = rest - part
        levels = jnp.where(lane == head + piece * HEADS, part, levels)
    wide = channels // LANES
    for block in range(blocks):
        span = slice(block * HEADS, (block + 1) * HEADS)
        summed = jnp.sum(weighted[span], axis=0, keepdims=True)
        for part in range(wide):
            row = block * wide + part
            slots[row : row + 1, :] = summed[:, part * LANES : (part + 1) * LANES]
        row = blocks * wide + block
        slots[row : row + 1, :] = jnp.sum(levels[span], axis=0, keepdims=True)
    out_ref[...] = jnp.broadcast_to(slots[...].astype(BF16)[None], out_ref.shape)


def merged(gathered, pick, spread, channels, query_count):
    wide = channels // LANES
    listed = pick.shape[0] // (wide + 1)
    places = listed // query_count
    picked = jnp.dot(pick, gathered, preferred_element_type=F32)
    levels = jnp.dot(picked[wide * listed :].astype(BF16), spread, preferred_element_type=F32)
    sums = jnp.concatenate(
        [picked[part * listed : (part + 1) * listed] for part in range(wide)], axis=1
    )

    def place(value, index):
        return value[index * query_count : (index + 1) * query_count]

    top = functools.reduce(jnp.maximum, [place(levels, index) for index in range(places)])
    weights = [jnp.exp(place(levels, index) - top) for index in range(places)]
    total = sum(weights)
    attn = sum(weight * place(sums, index) for index, weight in enumerate(weights)) / total
    return attn.astype(BF16)


def project(state, w_query, head_dim):
    return (
        jnp.dot(state.astype(BF16), w_query, preferred_element_type=F32) * head_dim ** (-0.5)
    ).astype(BF16)


def early_kernel(
    x_cells,
    own_hbm,
    taps_hbm,
    w_query_hbm,
    w_key_hbm,
    w_value_hbm,
    w_out_hbm,
    mask_weight_hbm,
    mask_rows,
    mask_column,
    taps,
    w_query,
    w_key,
    w_value,
    w_out,
    mask_weight,
    sums,
    listed,
    pick,
    spread,
    own,
    arrived,
):
    per_plane = taps.shape[0] // 3
    middle, low, high = (pl.ds(index * per_plane, per_plane) for index in (1, 0, 2))
    moves = [(own_hbm, own)]
    moves += [(taps_hbm.at[part], taps.at[part]) for part in (middle, low, high)]
    moves += [
        (w_query_hbm, w_query),
        (w_key_hbm, w_key),
        (w_value_hbm, w_value),
        (w_out_hbm, w_out),
        (mask_weight_hbm, mask_weight),
    ]
    copies = [
        pltpu.make_async_copy(source, target, arrived.at[index])
        for index, (source, target) in enumerate(moves)
    ]
    for copy in copies:
        copy.start()
    row_cells, _, channels = own.shape
    blocks = row_cells
    wide = channels // LANES
    query_count = mask_rows.shape[1]
    base = (lax.axis_index("span") * lax.axis_size("qry") + lax.axis_index("qry")) * blocks
    block_of_row = base + iota(listed.shape, 0) // HEADS
    hit = mask_rows[0:1, :] == block_of_row
    for place in range(1, mask_rows.shape[0]):
        hit = hit | (mask_rows[place : place + 1, :] == block_of_row)
    listed[...] = hit.astype(F32).astype(BF16)
    wanted = mask_column[...]
    many = wanted.shape[0]
    first_slot = wanted // blocks * SLOTS
    local_block = wanted % blocks
    slot = iota((many, pick.shape[1]), 1)
    for part in range(wide):
        target = first_slot + local_block * wide + part
        pick[part * many : (part + 1) * many, :] = (slot == target).astype(F32).astype(BF16)
    target = first_slot + blocks * wide + local_block
    pick[wide * many :, :] = (slot == target).astype(F32).astype(BF16)
    lane = iota(spread.shape, 0)
    head = iota(spread.shape, 1) // (channels // HEADS)
    spread[...] = ((lane % HEADS == head) & (lane < PIECES * HEADS)).astype(F32).astype(BF16)
    copies[0].wait()
    copies[1].wait()
    for x_off in range(3):
        total = None
        for row_off in range(3):
            rows = []
            for row in range(row_cells):
                source = row + row_off - 1
                if 0 <= source < row_cells:
                    rows.append(own[source])
                else:
                    rows.append(jnp.zeros(own.shape[1:], BF16))
            slab = jnp.concatenate(rows, axis=0)
            product = jnp.dot(
                slab, taps[per_plane + 3 * row_off + x_off], preferred_element_type=F32
            )
            total = product if total is None else total + product
        sums[x_off] = total
    for copy in copies[2:]:
        copy.wait()


def conv_kernel(sides, *refs):
    (plane_even, plane_odd, *rest) = refs
    halos = rest[: 3 * sides]
    (taps, sums_in, queries, peers, w_query, w_key, w_value, listed) = rest[
        3 * sides : 3 * sides + 8
    ]
    (pixel, states, parts, cells, slots) = rest[3 * sides + 8 :]
    row_cells, x_cells, channels = plane_even.shape
    row_id = lax.axis_index("qry")
    odd = lax.axis_index("span") % 2
    even_plane = 2 - 2 * odd
    odd_plane = 2 * odd
    blank = jnp.zeros((x_cells, channels), BF16)
    for depth_off in range(3):
        cells[depth_off, 0] = blank
        cells[depth_off, row_cells + 1] = blank
    for row in range(row_cells):
        cells[1, row + 1] = blank
        cells[even_plane, row + 1] = plane_even[row]
        cells[odd_plane, row + 1] = plane_odd[row]
    low = row_id % 2 == 0
    for parity in range(sides):
        at_end = low if parity == 0 else jnp.logical_not(low)
        row = jnp.where(at_end, row_cells + 1, 0)
        cells[1, row] = halos[3 * parity][...]
        cells[even_plane, row] = halos[3 * parity + 1][...]
        cells[odd_plane, row] = halos[3 * parity + 2][...]
    voxels = row_cells * x_cells
    sums = [sums_in[x_off] for x_off in range(3)]
    for depth_off in (0, 2, 1):
        for row_off in (0, 2) if depth_off == 1 else range(3):
            slab = cells[depth_off, row_off : row_off + row_cells].reshape(voxels, channels)
            for x_off in range(3):
                sums[x_off] = sums[x_off] + jnp.dot(
                    slab, taps[9 * depth_off + 3 * row_off + x_off], preferred_element_type=F32
                )
    x_id = iota((voxels, channels), 0) % x_cells
    conv = (
        sums[1]
        + jnp.where(x_id == 0, 0.0, pltpu.roll(sums[0], 1, 0))
        + jnp.where(x_id == x_cells - 1, 0.0, pltpu.roll(sums[2], voxels - 1, 0))
    )
    flat = jnp.maximum(conv, 0.0).astype(BF16)
    pixel[...] = flat
    here = queries.shape[0]
    if peers.shape[0] == states.shape[0]:
        states[...] = peers[...]
    else:
        states[pl.ds(pl.multiple_of(row_id * here, here), here), :] = queries[...]
        states[pl.ds(pl.multiple_of((1 - row_id) * here, here), here), :] = peers[...]
    qproj = project(states[...], w_query[0], channels // HEADS)
    keys = jnp.dot(flat, w_key[0], preferred_element_type=F32).astype(BF16)
    values = jnp.dot(flat, w_value[0], preferred_element_type=F32).astype(BF16)
    slots[...] = jnp.zeros(slots.shape, F32)
    partials(qproj, keys, values, listed[...], x_cells, slots, parts)


def layer_kernel(
    layer,
    x_cells,
    pixel,
    states,
    gathered,
    w_out,
    w_query,
    w_key,
    w_value,
    listed,
    pick,
    spread,
    new_states,
    parts,
    slots,
):
    channels = pixel.shape[1]
    flat = pixel[...]
    keys = jnp.dot(flat, w_key[layer], preferred_element_type=F32).astype(BF16)
    values = jnp.dot(flat, w_value[layer], preferred_element_type=F32).astype(BF16)
    attn = merged(gathered[...], pick[...], spread[...], channels, states.shape[0])
    state = states[...] + jnp.dot(attn, w_out[layer - 1], preferred_element_type=F32)
    new_states[...] = state
    qproj = project(state, w_query[layer], channels // HEADS)
    slots[...] = jnp.zeros(slots.shape, F32)
    partials(qproj, keys, values, listed[...], x_cells, slots, parts)


def final_kernel(
    x_cells,
    pixel,
    states,
    gathered,
    w_out,
    norm_gain,
    mask_weight,
    pick,
    spread,
    embed,
    logits,
    all_rows,
):
    voxels, channels = pixel.shape
    attn = merged(gathered[...], pick[...], spread[...], channels, states.shape[0])
    state = states[...] + jnp.dot(attn, w_out[LAYERS - 1], preferred_element_type=F32)
    mean = jnp.mean(state, axis=-1, keepdims=True)
    centered = state - mean
    var = jnp.mean(centered * centered, axis=-1, keepdims=True)
    query_embed = centered * lax.rsqrt(var + 1e-05) * norm_gain[...]
    all_rows[...] = query_embed
    here = embed.shape[0]
    embed[...] = all_rows[pl.ds(pl.multiple_of(lax.axis_index("qry") * here, here), here), :]
    mask_embed = jnp.dot(
        query_embed.astype(BF16), mask_weight[...], preferred_element_type=F32
    ).astype(BF16)
    scores = lax.dot_general(
        mask_embed, pixel[...], (((1,), (1,)), ((), ())), preferred_element_type=F32
    ) * channels ** (-0.5)
    for block in range(voxels // x_cells):
        logits[:, block, :] = scores[:, block * x_cells : (block + 1) * x_cells].astype(BF16)


def shape(dims, dtype):
    return jax.ShapeDtypeStruct(dims, dtype)


VMEM = pl.BlockSpec(memory_space=pltpu.VMEM)
HBM = pl.BlockSpec(memory_space=pltpu.HBM)


def grant(mebibytes):
    return pltpu.CompilerParams(vmem_limit_bytes=mebibytes << 20)


def kernel(body, outs, ins, scratch, room, name):
    return pl.pallas_call(
        body,
        out_shape=outs,
        in_specs=ins,
        out_specs=[VMEM] * len(outs),
        scratch_shapes=scratch,
        compiler_params=grant(room),
        name=name,
    )


def exchange(parts):
    gathered = lax.all_to_all(parts, AXES, split_axis=0, concat_axis=0, tiled=True)
    return gathered.reshape(-1, LANES)


def local(
    counts,
    features,
    conv_weight,
    queries,
    w_query,
    w_key,
    w_value,
    w_out,
    norm_gain,
    mask_weight,
    mask_blocks,
):
    depth_cells, row_cells, x_cells, channels = features.shape
    assert depth_cells == 1
    devices = counts[0] * counts[1]
    query_count, places = mask_blocks.shape
    voxels = row_cells * x_cells
    wide = channels // LANES
    assert row_cells * (wide + 1) <= SLOTS
    rows = row_cells * HEADS
    listed_count = query_count * places
    own = features[0]
    plane_odd = swap(own, counts, (1, None))
    plane_even = swap(own, counts, (0, None))
    row_low = lax.axis_index("qry") % 2 == 0
    halos = []
    parities = (0,) if counts[1] == 2 else (0, 1)
    for parity in parities:
        at_end = row_low if parity == 0 else jnp.logical_not(row_low)
        edge = lax.dynamic_index_in_dim(
            own, jnp.where(at_end, row_cells - 1, 0), axis=0, keepdims=False
        )
        for depth_parity in (None, 0, 1):
            halos.append(swap(edge, counts, (depth_parity, parity)))
    if counts[1] == 2:
        peers = swap(queries, counts, (None, 0))
    else:
        peers = lax.all_gather(queries, "qry", axis=0, tiled=True)
    mask_rows = mask_blocks.T
    mask_column = mask_rows.reshape(listed_count, 1)
    constant = [own, conv_weight, w_query, w_key, w_value, w_out, mask_weight]
    constant = [pltpu.with_memory_space_constraint(value, pltpu.HBM) for value in constant]
    (taps, w_query, w_key, w_value, w_out, mask_weight, sums, listed, pick, spread) = kernel(
        functools.partial(early_kernel, x_cells),
        [shape(value.shape, value.dtype) for value in constant[1:]]
        + [
            shape((3, voxels, channels), F32),
            shape((rows, query_count), BF16),
            shape(((wide + 1) * listed_count, devices * SLOTS), BF16),
            shape((LANES, channels), BF16),
        ],
        [HBM] * len(constant) + [VMEM] * 2,
        [pltpu.VMEM(own.shape, BF16), pltpu.SemaphoreType.DMA((9,))],
        24,
        "early",
    )(*constant, mask_rows, mask_column)
    parts_shape = shape((devices, SLOTS, LANES), BF16)
    slots = pltpu.VMEM((SLOTS, LANES), F32)
    states_shape = shape((query_count, channels), F32)
    pixel, states, parts = kernel(
        functools.partial(conv_kernel, len(parities)),
        [shape((voxels, channels), BF16), states_shape, parts_shape],
        [VMEM] * (10 + len(halos)),
        [pltpu.VMEM((3, row_cells + 2, x_cells, channels), BF16), slots],
        12,
        "conv_partials",
    )(
        plane_even,
        plane_odd,
        *halos,
        taps,
        sums,
        queries,
        peers,
        w_query,
        w_key,
        w_value,
        listed,
    )
    for layer in range(1, LAYERS):
        states, parts = kernel(
            functools.partial(layer_kernel, layer, x_cells),
            [states_shape, parts_shape],
            [VMEM] * 10,
            [slots],
            16,
            "layer_partials",
        )(
            pixel,
            states,
            exchange(parts),
            w_out,
            w_query,
            w_key,
            w_value,
            listed,
            pick,
            spread,
        )
    embed, logits = kernel(
        functools.partial(final_kernel, x_cells),
        [shape(queries.shape, F32), shape((query_count, row_cells, x_cells), BF16)],
        [VMEM] * 8,
        [pltpu.VMEM((query_count, channels), F32)],
        16,
        "final_logits",
    )(
        pixel,
        states,
        exchange(parts),
        w_out,
        norm_gain.reshape(1, channels),
        mask_weight,
        pick,
        spread,
    )
    return embed, logits.reshape(query_count, depth_cells, row_cells, x_cells)


def solution(mesh):
    counts = (mesh.shape["span"], mesh.shape["qry"])
    return jax.shard_map(
        functools.partial(local, counts),
        mesh=mesh,
        in_specs=(
            P("span", "qry", None, None),
            P(),
            P("qry", None),
            P(),
            P(),
            P(),
            P(),
            P(),
            P(),
            P(),
        ),
        out_specs=(P("qry", None), P(None, "span", "qry", None)),
        check_vma=False,
    )
```
